32 devices in a mesh: groups: 2 (over y), seq: 4 (over z), head: 4 (over x, core).
Axes of the slice: x: 2, y: 2, z: 4, core: 2. Of those that a mesh axis runs over, the one named last changes fastest.
Arguments:
- prefill_query: bfloat16 [1024, 128, 192], P(('groups', 'seq'), 'head'), parts along dimension 0, may hold values from -12 to 12
- prompt_latents: bfloat16 [1024, 576], P(('groups', 'seq', 'head')), parts along dimension 0, may hold values from -6 to 6
- decode_query: bfloat16 [256, 128, 192], P(('groups', 'seq'), 'head'), parts along dimension 0, may hold values from -12 to 12
- sample_latent: bfloat16 [256, 576], P(('groups', 'seq')), parts along dimension 0, may hold values from -6 to 6
- sample_length: int32 [256], P(('groups', 'seq')), parts along dimension 0, may hold values from 128 to 512
- up_key: bfloat16 [128, 128, 512], P('head'), may hold values from -0.5 to 0.5
- up_value: bfloat16 [128, 512, 128], P('head'), may hold values from -0.25 to 0.25
- out_proj: bfloat16 [16384, 7168], P('head', 'seq'), may hold values from -0.046875 to 0.046875
Outputs:
- prefill_heads: bfloat16 [1024, 16384], P(('groups', 'seq'), 'head'), parts along dimension 0
- decode_out: bfloat16 [256, 7168], P(('groups', 'head'), 'seq'), parts along dimension 0
The draws below stay inside these ranges and needn't reach their ends.
There are 2 independent parts, one for each index of `groups`. The reference program is written for one: setup_inputs(seed, part) draws one part's arguments, and reference() takes and returns one part's arrays. A program takes and returns all parts, laid end to end along the dimension named above; an argument that names none is the same for every part. Nothing has to cross between parts.
All inputs are finite; a program needn't handle non-finite values.
Results may differ from the reference program's by a relative error of at most 0.018.
Values may be sent and summed in bfloat16 or wider, within the bound.
A program may use at most 64 MiB of HBM per device.

```python
import jax
import jax.numpy as jnp
from jax import lax

D = 7168
HEADS = 128
NOPE = 128
ROPE = 64
KV_RANK = 512
VDIM = 128
S = 512
B = 128


def drawn_query(key, rows):
    base = jnp.clip(jax.random.normal(key, (rows, HEADS, NOPE + ROPE), jnp.float32), -6.0, 6.0)
    return base.astype(jnp.bfloat16)


def draw_prefill_query(key, part):
    return drawn_query(jax.random.fold_in(key, 1), S)


def draw_decode_query(key, part):
    return drawn_query(jax.random.fold_in(key, 2), B)


def draw_prompt_latents(key, part):
    base = jnp.clip(jax.random.normal(jax.random.fold_in(key, 3), (S, KV_RANK + ROPE), jnp.float32), -6.0, 6.0)
    return base.astype(jnp.bfloat16)


def with_ends(array, stream_key, low, top_value):
    longest = array.shape.index(max(array.shape))
    spots = []
    for shift in (0, 1):
        where = [jax.random.randint(jax.random.fold_in(stream_key, axis), (), 0, length) for axis, length in enumerate(array.shape)]
        where[longest] = (where[longest] + shift) % array.shape[longest]
        spots.append(tuple(where))
    return array.at[spots[0]].set(low).at[spots[1]].set(top_value)


def block_scale(key, dims, pieces, least, high):
    loudness, own = 1.0, jax.random.fold_in(key, 6)
    for axis_at, parts in pieces:
        steps = jnp.exp(jax.random.uniform(jax.random.fold_in(own, axis_at), (parts,), jnp.float32, least / len(pieces), high / len(pieces)))
        loudness = loudness * jnp.repeat(steps, dims[axis_at] // parts).reshape([-1 if axis == axis_at else 1 for axis in range(len(dims))])
    return loudness


def normal_values(key, extent, scale, bound, pieces=(), kind=jnp.bfloat16):
    level = block_scale(key, extent, pieces, -0.22, 0.18) if pieces else 1.0
    values = jax.random.normal(key, extent, jnp.float32) * scale * level
    return jnp.minimum(jnp.maximum(values, -bound), bound).astype(kind)


def setup_inputs(seed: int = 0, part: int = 0) -> dict:
    seeds = jax.random.split(jax.random.key(seed), 9)
    part_keys = jax.random.split(jax.random.fold_in(seeds[8], part), 9)
    prefill_query = draw_prefill_query(jax.random.fold_in(jax.random.fold_in(seeds[8], part), 71), part)
    prompt_latents = draw_prompt_latents(jax.random.fold_in(jax.random.fold_in(seeds[8], part), 71), part)
    decode_query = draw_decode_query(jax.random.fold_in(jax.random.fold_in(seeds[8], part), 71), part)
    sample_latent = normal_values(part_keys[3], (B, KV_RANK + ROPE), 1.0, 6.0, ((0, 4),))
    sample_length = with_ends(jax.random.randint(part_keys[4], (B,), S // 4, S + 1), jax.random.fold_in(part_keys[4], 1), S // 4, S).astype(jnp.int32)
    up_key = normal_values(seeds[5], (HEADS, NOPE, KV_RANK), NOPE ** -0.5, 0.5, ((0, 4),))
    up_value = normal_values(seeds[6], (HEADS, KV_RANK, VDIM), KV_RANK ** -0.5, 0.25, ((0, 4),))
    out_proj = normal_values(seeds[7], (HEADS * VDIM, D), (HEADS * VDIM) ** -0.5, 0.046875, ((0, 4), (1, 4)))
    return {"prefill_query": prefill_query, "prompt_latents": prompt_latents, "decode_query": decode_query, "sample_latent": sample_latent, "sample_length": sample_length, "up_key": up_key, "up_value": up_value, "out_proj": out_proj}


def absorb(query, up_key):
    nope = jnp.einsum("rhn,hnc->rhc", query[:, :, :NOPE].astype(jnp.float32), up_key.astype(jnp.float32))
    return jnp.concatenate([nope.astype(jnp.bfloat16), query[:, :, NOPE:]], axis=2)


def reference(prefill_query, prompt_latents, decode_query, sample_latent, sample_length, up_key, up_value, out_proj):
    scale = (NOPE + ROPE) ** -0.5
    values_part = prompt_latents[:, :KV_RANK]
    prefill_abs = jnp.swapaxes(absorb(prefill_query, up_key), 0, 1)
    decode_abs = jnp.swapaxes(absorb(decode_query, up_key), 0, 1)
    positions = jnp.arange(S, dtype=jnp.int32)
    causal = positions[None, :] <= positions[:, None]
    visible = positions[None, :] < sample_length[:, None]
    own_values = sample_latent[:, :KV_RANK].astype(jnp.float32)

    def prefill_head(items):
        query, weight_v = items
        scores = jnp.dot(query, prompt_latents.T, preferred_element_type=jnp.float32) * scale
        scores = jnp.where(causal, scores, -1e30)
        peak = jnp.max(scores, axis=1)
        weights = jnp.where(causal, jnp.exp(scores - peak[:, None]), 0.0)
        total = jnp.sum(weights, axis=1)
        latent = jnp.dot(weights.astype(jnp.bfloat16), values_part, preferred_element_type=jnp.float32) / total[:, None]
        return jnp.dot(latent.astype(jnp.bfloat16), weight_v, preferred_element_type=jnp.float32).astype(jnp.bfloat16)

    def decode_head(items):
        query, weight_v = items
        scores = jnp.dot(query, prompt_latents.T, preferred_element_type=jnp.float32) * scale
        scores = jnp.where(visible, scores, -1e30)
        own = jnp.sum(query.astype(jnp.float32) * sample_latent.astype(jnp.float32), axis=1) * scale
        peak = jnp.maximum(jnp.max(scores, axis=1), own)
        weights = jnp.where(visible, jnp.exp(scores - peak[:, None]), 0.0)
        own_weight = jnp.exp(own - peak)
        total = jnp.sum(weights, axis=1) + own_weight
        latent = jnp.dot(weights.astype(jnp.bfloat16), values_part, preferred_element_type=jnp.float32)
        latent = (latent + own_weight[:, None] * own_values) / total[:, None]
        return jnp.dot(latent.astype(jnp.bfloat16), weight_v, preferred_element_type=jnp.float32).astype(jnp.bfloat16)

    prefill_out = lax.map(prefill_head, (prefill_abs, up_value))
    prefill_heads = jnp.swapaxes(prefill_out, 0, 1).reshape(S, HEADS * VDIM)
    decode_vals = lax.map(decode_head, (decode_abs, up_value))
    sample_heads = jnp.swapaxes(decode_vals, 0, 1).reshape(B, HEADS * VDIM)
    decode_out = jnp.dot(sample_heads, out_proj, preferred_element_type=jnp.float32).astype(jnp.bfloat16)
    return prefill_heads, decode_out
```

```python
import functools

import jax
import jax.numpy as jnp
from jax import lax
from jax.experimental import pallas as pl
from jax.experimental.pallas import tpu as pltpu
from jax.sharding import PartitionSpec as P


def absorb(query, up_key, nope_width):
    nope = jnp.einsum(
        "rhn,hnc->rhc", query[:, :, :nope_width], up_key, preferred_element_type=jnp.float32
    )
    return jnp.concatenate([nope.astype(jnp.bfloat16), query[:, :, nope_width:]], axis=2)


def fold_block(state, queries, piece, allowed_fn, kv_width, scale):
    peak, total, summed = state
    key_pos = jnp.arange(piece.shape[0], dtype=jnp.int32)
    allowed = allowed_fn(key_pos)
    scores = (
        lax.dot_general(
            queries, piece, (((1,), (1,)), ((), ())), preferred_element_type=jnp.float32
        )
        * scale
    )
    scores = jnp.where(allowed, scores, -1e30)
    new_peak = jnp.maximum(peak, jnp.max(scores, axis=1))
    weights = jnp.where(allowed, jnp.exp(scores - new_peak[:, None]), 0.0)
    factor = jnp.exp(peak - new_peak)
    total = total * factor + jnp.sum(weights, axis=1)
    summed = summed * factor[:, None] + jnp.dot(
        weights.astype(jnp.bfloat16), piece[:, :kv_width], preferred_element_type=jnp.float32
    )
    return (new_peak, total, summed)


def finish(state, rows, head_count, up_value):
    peak, total, summed = state
    latent = (summed / total[:, None]).astype(jnp.bfloat16).reshape(rows, head_count, -1)
    heads = jnp.einsum("rhc,hcv->rhv", latent, up_value, preferred_element_type=jnp.float32)
    return heads.astype(jnp.bfloat16).reshape(rows, -1)


def plain_device(
    prefill_query,
    prompt_latents,
    decode_query,
    sample_latent,
    sample_length,
    up_key,
    up_value,
    out_proj,
):
    local_rows, head_count, query_width = prefill_query.shape
    sample_rows = decode_query.shape[0]
    nope_width = up_key.shape[1]
    kv_width = up_key.shape[2]
    scale = query_width ** (-0.5)
    block = lax.all_gather(prompt_latents, "head", axis=0, tiled=True)
    prefill_rows = absorb(prefill_query, up_key, nope_width).reshape(local_rows * head_count, -1)
    first = lax.axis_index("seq") * local_rows
    query_pos = first + jnp.arange(local_rows * head_count, dtype=jnp.int32) // head_count
    decode_abs = absorb(decode_query, up_key, nope_width)
    decode_rows = decode_abs.reshape(sample_rows * head_count, -1)
    row_length = jnp.repeat(sample_length, head_count)
    own = (
        jnp.einsum(
            "rhc,rc->rh", decode_abs, sample_latent, preferred_element_type=jnp.float32
        ).reshape(-1)
        * scale
    )
    own_values = jnp.repeat(sample_latent[:, :kv_width].astype(jnp.float32), head_count, axis=0)
    count_prefill = local_rows * head_count
    prefill_init = (
        jnp.full((count_prefill,), -1e30, jnp.float32),
        jnp.zeros((count_prefill,), jnp.float32),
        jnp.zeros((count_prefill, kv_width), jnp.float32),
    )
    decode_init = (own, jnp.ones_like(own), own_values)

    def prefill_inner(state, piece):
        return fold_block(
            state,
            prefill_rows,
            piece,
            lambda key_pos: key_pos[None, :] <= query_pos[:, None],
            kv_width,
            scale,
        )

    def decode_inner(state, piece):
        return fold_block(
            state,
            decode_rows,
            piece,
            lambda key_pos: key_pos[None, :] < row_length[:, None],
            kv_width,
            scale,
        )

    def prefill_step(state, piece):
        return prefill_inner(state, piece)

    def decode_step(state, piece):
        return decode_inner(state, piece)

    state = (prefill_init, decode_init)
    piece = lax.all_gather(block, "seq", axis=0, tiled=True)
    prefill_state = prefill_step(state[0], piece)
    decode_state = decode_step(state[1], piece)
    prefill_heads = finish(prefill_state, local_rows, head_count, up_value)
    sample_heads = finish(decode_state, sample_rows, head_count, up_value)
    terms = jnp.dot(
        lax.all_gather(sample_heads, "seq", axis=0, tiled=True),
        out_proj,
        preferred_element_type=jnp.float32,
    )
    decode_out = lax.psum_scatter(
        terms.astype(jnp.bfloat16), "head", scatter_dimension=0, tiled=True
    )
    return (prefill_heads, decode_out)


LANES = 128
MASKED = -1e30
BF16 = jnp.bfloat16
F32 = jnp.float32


def round_up(value, unit):
    return -(-value // unit) * unit


def softmax_latent(queries, keys_t, values, bias, scale):
    rows = queries.shape[0]
    scores = jnp.dot(queries, keys_t, preferred_element_type=F32)
    per_head, key_count = bias.shape
    scores = (scores.reshape(rows // per_head, per_head, key_count) + bias[None]).reshape(
        rows, key_count
    )
    peak = jnp.max(scores, axis=1, keepdims=True)
    weights = jnp.exp((scores - peak) * scale)
    total = jnp.sum(weights, axis=1, keepdims=True)
    summed = jnp.dot(weights.astype(BF16), values, preferred_element_type=F32)
    return (summed * (1.0 / total)).astype(BF16)


def step_kernel(
    cfg,
    pq_hbm,
    lat_hbm,
    dq_hbm,
    own_ref,
    len_ref,
    upk_hbm,
    upv_hbm,
    proj_hbm,
    out_hbm,
    dec_ref,
    pq,
    dq,
    lat,
    upk,
    upv,
    proj,
    nope_rows,
    rope_rows,
    pre_abs,
    dec_abs,
    keys,
    keys_t,
    pre_bias,
    dec_bias,
    heads,
    out,
    terms,
    arrived,
    pq_sem,
    dq_sem,
    lat_sem,
    upk_sem,
    upv_sem,
    proj_sem,
    out_sem,
    z_send,
    z_recv,
    x_send,
    x_recv,
    c_send,
    c_recv,
    h_send,
    h_recv,
    r_send,
    r_recv,
):
    ns, nh, scale = cfg["ns"], cfg["nh"], cfg["scale"]
    rows, hc, width = pq.shape
    samples = dq.shape[0]
    nope, kv = upk.shape[1], upk.shape[2]
    vdim = upv.shape[2]
    rope = width - nope
    lat_width = lat.shape[2]
    block = lat.shape[1]
    prompt = ns * nh * block
    padded = keys.shape[1]
    nx = nh // 2
    z, hd = lax.axis_index("seq"), lax.axis_index("head")
    core_peer = hd + 1 - 2 * lax.rem(hd, 2)

    def seq_peer(d):
        return lax.rem(z + d, ns)

    def head_peer(d):
        return lax.rem(hd + d, nh)

    copies = {}
    copies["pq"] = pltpu.make_async_copy(pq_hbm, pq, pq_sem)
    copies["dq"] = pltpu.make_async_copy(dq_hbm, dq, dq_sem)
    me_block = z * nh + hd
    copies["lat"] = pltpu.make_async_copy(lat_hbm, lat.at[me_block], lat_sem)
    chunks = cfg["chunks"]
    per_chunk = hc // chunks
    copies["lat"].start()
    copies["pq"].start()
    copies["dq"].start()
    upk_copies = [
        pltpu.make_async_copy(
            upk_hbm.at[pl.ds(c * per_chunk, per_chunk)],
            upk.at[pl.ds(c * per_chunk, per_chunk)],
            upk_sem.at[c],
        )
        for c in range(chunks)
    ]
    for copy in upk_copies:
        copy.start()
    upv_copy = pltpu.make_async_copy(upv_hbm, upv, upv_sem)
    upv_copy.start()
    proj_copy = pltpu.make_async_copy(proj_hbm, proj, proj_sem)
    proj_copy.start()

    barrier = pltpu.get_barrier_semaphore()
    for d in range(1, ns):
        pl.semaphore_signal(barrier, inc=1, device_id={"seq": seq_peer(d)})
    for d in range(1, nh):
        pl.semaphore_signal(barrier, inc=1, device_id={"head": head_peer(d)})
    pl.semaphore_wait(barrier, ns + nh - 2)

    sent = []

    def send(src, dst, send_sem, recv_sem, device):
        copy = pltpu.make_async_remote_copy(
            src_ref=src, dst_ref=dst, send_sem=send_sem, recv_sem=recv_sem, device_id=device
        )
        copy.start()
        sent.append(copy)

    def received(dst, recv_sem, send_sem, device):
        pltpu.make_async_remote_copy(
            src_ref=dst, dst_ref=dst, send_sem=send_sem, recv_sem=recv_sem, device_id=device
        ).wait_recv()

    def lat_block(d, j):
        return lax.rem(z - d + ns, ns) * nh + lax.rem(hd - 2 * j + nh, nh)

    def to_core(d, j):
        slot = lat.at[lat_block(d, j)]
        send(slot, slot, c_send.at[d, j], c_recv.at[d, j], {"head": core_peer})

    def to_x(d):
        slot = lat.at[lat_block(d, 0)]
        for j in range(1, nx):
            send(slot, slot, x_send.at[d, j], x_recv.at[d, j], {"head": head_peer(2 * j)})

    copies["lat"].wait()
    mine = lat.at[me_block]
    order = sorted(range(1, ns), key=lambda d: min(d, ns - d))
    for d in order:
        send(mine, mine, z_send.at[d], z_recv.at[d], {"seq": seq_peer(d)})
    to_x(0)
    to_core(0, 0)

    def take_z(d):
        received(lat.at[lat_block(d, 0)], z_recv.at[d], z_send.at[d], {"seq": seq_peer(d)})
        to_x(d)
        to_core(d, 0)

    def take_x(d):
        for j in range(1, nx):
            received(
                lat.at[lat_block(d, j)], x_recv.at[d, j], x_send.at[d, j], {"head": core_peer}
            )
            to_core(d, j)

    rope_rows[...] = jnp.zeros_like(rope_rows)
    copies["pq"].wait()
    copies["dq"].wait()

    def spread(source, base, count):
        step = 8

        def body(i, carry):
            piece = source[pl.ds(i * step, step)].astype(F32)
            at = pl.multiple_of(base * hc + i * step * hc, 8)
            nope_rows[pl.ds(at, step * hc), :] = piece[:, :, :nope].reshape(step * hc, nope)
            rope_rows[pl.ds(at, step * hc), 0:rope] = piece[:, :, nope:].reshape(step * hc, rope)
            return carry

        lax.fori_loop(0, count // step, body, 0)

    spread(pq, 0, rows)
    spread(dq, rows, samples)

    def absorb_head(h, carry):
        take = pl.ds(h, rows + samples, stride=hc)
        plain = nope_rows[take, :].astype(BF16)
        turned = rope_rows[take, :].astype(BF16)
        absorbed = jnp.dot(plain, upk[h], preferred_element_type=F32).astype(BF16)
        at = pl.multiple_of(h * rows, 16)
        pre_abs[pl.ds(at, rows), 0:kv] = absorbed[:rows]
        pre_abs[pl.ds(at, rows), kv:padded] = turned[:rows]
        at = pl.multiple_of(h * samples, 16)
        dec_abs[pl.ds(at, samples), 0:kv] = absorbed[rows:]
        dec_abs[pl.ds(at, samples), kv:padded] = turned[rows:]
        return carry

    pending = [functools.partial(take_z, d) for d in order]
    pending += [functools.partial(take_x, d) for d in [0] + order]
    share = -(-len(pending) // max(chunks - 1, 1))
    for c in range(chunks):
        upk_copies[c].wait()
        lax.fori_loop(c * per_chunk, (c + 1) * per_chunk, absorb_head, 0, unroll=2)
        for action in pending[:share]:
            action()
        pending = pending[share:]
    for action in pending:
        action()

    key_at = lax.broadcasted_iota(jnp.int32, (rows, prompt), 1)
    query_at = z * rows + lax.broadcasted_iota(jnp.int32, (rows, prompt), 0)
    pre_bias[...] = jnp.where(key_at <= query_at, 0.0, MASKED)
    key_at = lax.broadcasted_iota(jnp.int32, dec_bias.shape, 1)
    own_at = prompt + lax.broadcasted_iota(jnp.int32, dec_bias.shape, 0)
    dec_bias[...] = jnp.where((key_at < len_ref[...]) | (key_at == own_at), 0.0, MASKED)

    keys[...] = jnp.zeros_like(keys)
    keys[prompt : prompt + samples, 0:lat_width] = own_ref[...]
    for d in range(ns):
        for j in range(nx):
            at = lax.rem(z - d + ns, ns) * nh + lax.rem(core_peer - 2 * j + nh, nh)
            received(lat.at[at], c_recv.at[d, j], c_send.at[d, j], {"head": core_peer})
    for i in range(ns * nh):
        keys[i * block : (i + 1) * block, 0:lat_width] = lat[i]
    keys_t[...] = keys[...].T

    upv_copy.wait()
    dec_heads = cfg["dec_heads"]

    def decode_group(g, carry):
        at = pl.multiple_of(g * dec_heads * samples, 16)
        latent = softmax_latent(
            dec_abs[pl.ds(at, dec_heads * samples), :],
            keys_t[...],
            keys[:, 0:kv],
            dec_bias[...],
            scale,
        )
        for i in range(dec_heads):
            h = g * dec_heads + i
            one = jnp.dot(
                latent[i * samples : (i + 1) * samples], upv[h], preferred_element_type=F32
            )
            heads[z, :, pl.ds(pl.multiple_of(h * vdim, vdim), vdim)] = one.astype(BF16)
        return carry

    lax.fori_loop(0, hc // dec_heads, decode_group, 0)
    for d in order:
        slot = heads.at[z]
        send(slot, slot, h_send.at[d], h_recv.at[d], {"seq": seq_peer(d)})

    pre_heads = cfg["pre_heads"]
    groups = hc // pre_heads
    group_cols = pre_heads * vdim

    def prefill_group(g, carry):
        at = pl.multiple_of(g * pre_heads * rows, 16)
        latent = softmax_latent(
            pre_abs[pl.ds(at, pre_heads * rows), :],
            keys_t[:, 0:prompt],
            keys[0:prompt, 0:kv],
            pre_bias[...],
            scale,
        )
        for i in range(pre_heads):
            h = g * pre_heads + i
            one = jnp.dot(latent[i * rows : (i + 1) * rows], upv[h], preferred_element_type=F32)
            out[:, pl.ds(pl.multiple_of(h * vdim, vdim), vdim)] = one.astype(BF16)
        return carry

    first = groups // 2
    half_cols = first * group_cols
    lax.fori_loop(0, first, prefill_group, 0)
    front = pltpu.make_async_copy(
        out.at[:, pl.ds(0, half_cols)], out_hbm.at[:, pl.ds(0, half_cols)], out_sem.at[0]
    )
    front.start()

    proj_copy.wait()
    for d in order:
        at = lax.rem(z - d + ns, ns)
        received(heads.at[at], h_recv.at[d], h_send.at[d], {"seq": seq_peer(d)})
    cols = proj.shape[1]
    tile = cfg["tile"]
    share_rows = ns * samples // nh

    def project(n, carry):
        take = pl.ds(pl.multiple_of(n * tile, tile), tile)
        left = heads[...].reshape(ns * samples, hc * vdim)
        term = jnp.dot(left, proj[:, take], preferred_element_type=F32).astype(BF16)
        terms[:, :, take] = term.reshape(nh, share_rows, tile)
        return carry

    lax.fori_loop(0, cols // tile, project, 0)
    for d in range(1, nh):
        peer = head_peer(d)
        send(terms.at[peer], arrived.at[d], r_send.at[d], r_recv.at[d], {"head": peer})

    lax.fori_loop(first, groups, prefill_group, 0)
    back_cols = out.shape[1] - half_cols
    back = pltpu.make_async_copy(
        out.at[:, pl.ds(half_cols, back_cols)],
        out_hbm.at[:, pl.ds(half_cols, back_cols)],
        out_sem.at[1],
    )
    back.start()
    total = terms[hd].astype(F32)
    for d in range(1, nh):
        received(arrived.at[d], r_recv.at[d], r_send.at[d], {"head": core_peer})
        total = total + arrived[d].astype(F32)
    dec_ref[...] = total.astype(BF16)
    front.wait()
    back.wait()
    for copy in sent:
        copy.wait_send()


def fused_device(ns, nh, pq, lat, dq, own, length, upk, upv, proj):
    rows, hc, width = pq.shape
    samples = dq.shape[0]
    nope, kv = upk.shape[1:]
    vdim = upv.shape[2]
    block, lat_width = lat.shape
    prompt = ns * nh * block
    padded = round_up(lat_width, LANES)
    cols = proj.shape[1]
    share_rows = ns * samples // nh
    keys_rows = prompt + round_up(samples, LANES)
    nx = nh // 2
    dec_heads = max(1, min(hc, 512 // samples))
    pre_heads = max(1, min(hc // 2, 512 // rows))
    cfg = {
        "ns": ns,
        "nh": nh,
        "scale": width ** (-0.5),
        "chunks": 4,
        "dec_heads": dec_heads,
        "pre_heads": pre_heads,
        "tile": 256 if cols % 256 == 0 else LANES,
    }
    hbm = pl.BlockSpec(memory_space=pl.ANY)
    vmem = pl.BlockSpec(memory_space=pltpu.VMEM)
    dma = pltpu.SemaphoreType.DMA
    return pl.pallas_call(
        functools.partial(step_kernel, cfg),
        out_shape=(
            jax.ShapeDtypeStruct((rows, hc * vdim), BF16),
            jax.ShapeDtypeStruct((share_rows, cols), BF16),
        ),
        in_specs=[hbm, hbm, hbm, vmem, vmem, hbm, hbm, hbm],
        out_specs=(hbm, vmem),
        scratch_shapes=[
            pltpu.VMEM((rows, hc, width), BF16),
            pltpu.VMEM((samples, hc, width), BF16),
            pltpu.VMEM((ns * nh, block, lat_width), BF16),
            pltpu.VMEM((hc, nope, kv), BF16),
            pltpu.VMEM((hc, kv, vdim), BF16),
            pltpu.VMEM(proj.shape, BF16),
            pltpu.VMEM(((rows + samples) * hc, nope), F32),
            pltpu.VMEM(((rows + samples) * hc, LANES), F32),
            pltpu.VMEM((rows * hc, padded), BF16),
            pltpu.VMEM((samples * hc, padded), BF16),
            pltpu.VMEM((keys_rows, padded), BF16),
            pltpu.VMEM((padded, keys_rows), BF16),
            pltpu.VMEM((rows, prompt), F32),
            pltpu.VMEM((samples, keys_rows), F32),
            pltpu.VMEM((ns, samples, hc * vdim), BF16),
            pltpu.VMEM((rows, hc * vdim), BF16),
            pltpu.VMEM((nh, share_rows, cols), BF16),
            pltpu.VMEM((nh, share_rows, cols), BF16),
            dma,
            dma,
            dma,
            dma((cfg["chunks"],)),
            dma,
            dma,
            dma((2,)),
            dma((ns,)),
            dma((ns,)),
            dma((ns, nx)),
            dma((ns, nx)),
            dma((ns, nx)),
            dma((ns, nx)),
            dma((ns,)),
            dma((ns,)),
            dma((nh,)),
            dma((nh,)),
        ],
        compiler_params=pltpu.CompilerParams(
            collective_id=0, has_side_effects=True, vmem_limit_bytes=62 * 1024 * 1024
        ),
        name="rollout_step",
    )(pq, lat, dq, own, length.reshape(samples, 1), upk, upv, proj)


def per_device(ns, nh, *args):
    pq, lat, dq, own, length, upk, upv, proj = args
    samples, hc = dq.shape[:2]
    fits = (
        lat.shape[0] % 16 == 0
        and nh % 2 == 0
        and ns > 1
        and hc % 8 == 0
        and pq.shape[0] % 16 == 0
        and samples % 16 == 0
        and (ns * samples) % (nh * 16) == 0
        and upk.shape[1] == LANES
        and upk.shape[2] % LANES == 0
        and upv.shape[2] == LANES
        and proj.shape[1] % LANES == 0
        and (ns * nh * lat.shape[0]) % LANES == 0
    )
    if fits:
        return tuple(fused_device(ns, nh, *args))
    return plain_device(*args)


def solution(mesh):
    in_specs = (
        P(("groups", "seq"), "head", None),
        P(("groups", "seq", "head"), None),
        P(("groups", "seq"), "head", None),
        P(("groups", "seq"), None),
        P(("groups", "seq")),
        P("head", None, None),
        P("head", None, None),
        P("head", "seq"),
    )
    out_specs = (P(("groups", "seq"), "head"), P(("groups", "head"), "seq"))
    return jax.shard_map(
        functools.partial(per_device, mesh.shape["seq"], mesh.shape["head"]),
        mesh=mesh, in_specs=in_specs,
        out_specs=out_specs,
        check_vma=False
    )
```

```python
import functools

import jax
import jax.numpy as jnp
from jax import lax
from jax.experimental import pallas as pl
from jax.experimental.pallas import tpu as pltpu
from jax.sharding import PartitionSpec as P


def absorb(query, up_key, nope_width):
    nope = jnp.einsum(
        "rhn,hnc->rhc", query[:, :, :nope_width], up_key, preferred_element_type=jnp.float32
    )
    return jnp.concatenate([nope.astype(jnp.bfloat16), query[:, :, nope_width:]], axis=2)


def fold_block(state, queries, piece, allowed_fn, kv_width, scale):
    peak, total, summed = state
    key_pos = jnp.arange(piece.shape[0], dtype=jnp.int32)
    allowed = allowed_fn(key_pos)
    scores = (
        lax.dot_general(
            queries, piece, (((1,), (1,)), ((), ())), preferred_element_type=jnp.float32
        )
        * scale
    )
    scores = jnp.where(allowed, scores, -1e30)
    new_peak = jnp.maximum(peak, jnp.max(scores, axis=1))
    weights = jnp.where(allowed, jnp.exp(scores - new_peak[:, None]), 0.0)
    factor = jnp.exp(peak - new_peak)
    total = total * factor + jnp.sum(weights, axis=1)
    summed = summed * factor[:, None] + jnp.dot(
        weights.astype(jnp.bfloat16), piece[:, :kv_width], preferred_element_type=jnp.float32
    )
    return (new_peak, total, summed)


def finish(state, rows, head_count, up_value):
    peak, total, summed = state
    latent = (summed / total[:, None]).astype(jnp.bfloat16).reshape(rows, head_count, -1)
    heads = jnp.einsum("rhc,hcv->rhv", latent, up_value, preferred_element_type=jnp.float32)
    return heads.astype(jnp.bfloat16).reshape(rows, -1)


def plain_device(
    prefill_query,
    prompt_latents,
    decode_query,
    sample_latent,
    sample_length,
    up_key,
    up_value,
    out_proj,
):
    local_rows, head_count, query_width = prefill_query.shape
    sample_rows = decode_query.shape[0]
    nope_width = up_key.shape[1]
    kv_width = up_key.shape[2]
    scale = query_width ** (-0.5)
    block = lax.all_gather(prompt_latents, "head", axis=0, tiled=True)
    prefill_rows = absorb(prefill_query, up_key, nope_width).reshape(local_rows * head_count, -1)
    first = lax.axis_index("seq") * local_rows
    query_pos = first + jnp.arange(local_rows * head_count, dtype=jnp.int32) // head_count
    decode_abs = absorb(decode_query, up_key, nope_width)
    decode_rows = decode_abs.reshape(sample_rows * head_count, -1)
    row_length = jnp.repeat(sample_length, head_count)
    own = (
        jnp.einsum(
            "rhc,rc->rh", decode_abs, sample_latent, preferred_element_type=jnp.float32
        ).reshape(-1)
        * scale
    )
    own_values = jnp.repeat(sample_latent[:, :kv_width].astype(jnp.float32), head_count, axis=0)
    count_prefill = local_rows * head_count
    prefill_init = (
        jnp.full((count_prefill,), -1e30, jnp.float32),
        jnp.zeros((count_prefill,), jnp.float32),
        jnp.zeros((count_prefill, kv_width), jnp.float32),
    )
    decode_init = (own, jnp.ones_like(own), own_values)

    def prefill_inner(state, piece):
        return fold_block(
            state,
            prefill_rows,
            piece,
            lambda key_pos: key_pos[None, :] <= query_pos[:, None],
            kv_width,
            scale,
        )

    def decode_inner(state, piece):
        return fold_block(
            state,
            decode_rows,
            piece,
            lambda key_pos: key_pos[None, :] < row_length[:, None],
            kv_width,
            scale,
        )

    def prefill_step(state, piece):
        return prefill_inner(state, piece)

    def decode_step(state, piece):
        return decode_inner(state, piece)

    state = (prefill_init, decode_init)
    piece = lax.all_gather(block, "seq", axis=0, tiled=True)
    prefill_state = prefill_step(state[0], piece)
    decode_state = decode_step(state[1], piece)
    prefill_heads = finish(prefill_state, local_rows, head_count, up_value)
    sample_heads = finish(decode_state, sample_rows, head_count, up_value)
    terms = jnp.dot(
        lax.all_gather(sample_heads, "seq", axis=0, tiled=True),
        out_proj,
        preferred_element_type=jnp.float32,
    )
    decode_out = lax.psum_scatter(
        terms.astype(jnp.bfloat16), "head", scatter_dimension=0, tiled=True
    )
    return (prefill_heads, decode_out)


LANES = 128
MASKED = -1e30
BF16 = jnp.bfloat16
F32 = jnp.float32


def round_up(value, unit):
    return -(-value // unit) * unit


def softmax_latent(queries, keys_t, values, bias, scale):
    rows = queries.shape[0]
    scores = jnp.dot(queries, keys_t, preferred_element_type=F32)
    per_head, key_count = bias.shape
    scores = (scores.reshape(rows // per_head, per_head, key_count) + bias[None]).reshape(
        rows, key_count
    )
    peak = jnp.max(scores, axis=1, keepdims=True)
    weights = jnp.exp((scores - peak) * scale)
    total = jnp.sum(weights, axis=1, keepdims=True)
    summed = jnp.dot(weights.astype(BF16), values, preferred_element_type=F32)
    return (summed * (1.0 / total)).astype(BF16)


def step_kernel(
    cfg,
    pq_hbm,
    lat_hbm,
    dq_hbm,
    own_ref,
    len_ref,
    upk_hbm,
    upv_hbm,
    proj_hbm,
    out_hbm,
    dec_ref,
    pq,
    dq,
    lat,
    upk,
    upv,
    proj,
    nope_rows,
    rope_rows,
    pre_abs,
    dec_abs,
    keys,
    keys_t,
    pre_bias,
    dec_bias,
    heads,
    out,
    terms,
    arrived,
    pq_sem,
    dq_sem,
    lat_sem,
    upk_sem,
    upv_sem,
    proj_sem,
    out_sem,
    z_send,
    z_recv,
    x_send,
    x_recv,
    c_send,
    c_recv,
    h_send,
    h_recv,
    r_send,
    r_recv,
):
    ns, nh, scale = cfg["ns"], cfg["nh"], cfg["scale"]
    hc, width, rows = pq.shape
    samples = dq.shape[0]
    nope, kv = upk.shape[1], upk.shape[2]
    vdim = upv.shape[2]
    rope = width - nope
    lat_width = lat.shape[2]
    block = lat.shape[1]
    prompt = ns * nh * block
    padded = keys.shape[1]
    nx = nh // 2
    z, hd = lax.axis_index("seq"), lax.axis_index("head")
    core_peer = hd + 1 - 2 * lax.rem(hd, 2)

    def seq_peer(d):
        return lax.rem(z + d, ns)

    def head_peer(d):
        return lax.rem(hd + d, nh)

    copies = {}
    copies["pq"] = pltpu.make_async_copy(pq_hbm, pq, pq_sem)
    copies["dq"] = pltpu.make_async_copy(dq_hbm, dq, dq_sem)
    me_block = z * nh + hd
    copies["lat"] = pltpu.make_async_copy(lat_hbm, lat.at[me_block], lat_sem)
    chunks = cfg["chunks"]
    per_chunk = hc // chunks
    copies["lat"].start()
    copies["pq"].start()
    copies["dq"].start()
    upk_copies = [
        pltpu.make_async_copy(
            upk_hbm.at[pl.ds(c * per_chunk, per_chunk)],
            upk.at[pl.ds(c * per_chunk, per_chunk)],
            upk_sem.at[c],
        )
        for c in range(chunks)
    ]
    for copy in upk_copies:
        copy.start()
    upv_copy = pltpu.make_async_copy(upv_hbm, upv, upv_sem)
    upv_copy.start()
    proj_copy = pltpu.make_async_copy(proj_hbm, proj, proj_sem)
    proj_copy.start()

    barrier = pltpu.get_barrier_semaphore()
    for d in range(1, ns):
        pl.semaphore_signal(barrier, inc=1, device_id={"seq": seq_peer(d)})
    for d in range(1, nh):
        pl.semaphore_signal(barrier, inc=1, device_id={"head": head_peer(d)})
    pl.semaphore_wait(barrier, ns + nh - 2)

    sent = []

    def send(src, dst, send_sem, recv_sem, device):
        copy = pltpu.make_async_remote_copy(
            src_ref=src, dst_ref=dst, send_sem=send_sem, recv_sem=recv_sem, device_id=device
        )
        copy.start()
        sent.append(copy)

    def received(dst, recv_sem, send_sem, device):
        pltpu.make_async_remote_copy(
            src_ref=dst, dst_ref=dst, send_sem=send_sem, recv_sem=recv_sem, device_id=device
        ).wait_recv()

    def lat_block(d, j):
        return lax.rem(z - d + ns, ns) * nh + lax.rem(hd - 2 * j + nh, nh)

    def to_core(d, j):
        slot = lat.at[lat_block(d, j)]
        send(slot, slot, c_send.at[d, j], c_recv.at[d, j], {"head": core_peer})

    def to_x(d):
        slot = lat.at[lat_block(d, 0)]
        for j in range(1, nx):
            send(slot, slot, x_send.at[d, j], x_recv.at[d, j], {"head": head_peer(2 * j)})

    copies["lat"].wait()
    mine = lat.at[me_block]
    order = sorted(range(1, ns), key=lambda d: min(d, ns - d))
    for d in order:
        send(mine, mine, z_send.at[d], z_recv.at[d], {"seq": seq_peer(d)})
    to_x(0)
    to_core(0, 0)

    def take_z(d):
        received(lat.at[lat_block(d, 0)], z_recv.at[d], z_send.at[d], {"seq": seq_peer(d)})
        to_x(d)
        to_core(d, 0)

    def take_x(d):
        for j in range(1, nx):
            received(
                lat.at[lat_block(d, j)], x_recv.at[d, j], x_send.at[d, j], {"head": core_peer}
            )
            to_core(d, j)

    rope_rows[...] = jnp.zeros_like(rope_rows)
    pre_abs[:, kv:padded] = jnp.zeros((rows * hc, padded - kv), BF16)
    copies["dq"].wait()
    step = 8

    def spread(i, carry):
        piece = dq[pl.ds(i * step, step)].astype(F32)
        take = pl.ds(pl.multiple_of(i * step * hc, 8), step * hc)
        nope_rows[take, :] = piece[:, :, :nope].reshape(step * hc, nope)
        rope_rows[take, 0:rope] = piece[:, :, nope:].reshape(step * hc, rope)
        return carry

    lax.fori_loop(0, samples // step, spread, 0)
    copies["pq"].wait()

    def absorb_head(h, carry):
        query = pq[h].T
        take = pl.ds(h, samples, stride=hc)
        plain = jnp.concatenate([query[:, :nope], nope_rows[take, :].astype(BF16)], axis=0)
        turned = rope_rows[take, :].astype(BF16)
        absorbed = jnp.dot(plain, upk[h], preferred_element_type=F32).astype(BF16)
        at = pl.multiple_of(h * rows, 16)
        pre_abs[pl.ds(at, rows), 0:kv] = absorbed[:rows]
        pre_abs[pl.ds(at, rows), kv : kv + rope] = query[:, nope:]
        at = pl.multiple_of(h * samples, 16)
        dec_abs[pl.ds(at, samples), 0:kv] = absorbed[rows:]
        dec_abs[pl.ds(at, samples), kv:padded] = turned
        return carry

    pending = [functools.partial(take_z, d) for d in order]
    pending += [functools.partial(take_x, d) for d in [0] + order]
    share = -(-len(pending) // max(chunks - 1, 1))
    for c in range(chunks):
        upk_copies[c].wait()
        lax.fori_loop(c * per_chunk, (c + 1) * per_chunk, absorb_head, 0, unroll=2)
        for action in pending[:share]:
            action()
        pending = pending[share:]
    for action in pending:
        action()

    key_at = lax.broadcasted_iota(jnp.int32, (rows, prompt), 1)
    query_at = z * rows + lax.broadcasted_iota(jnp.int32, (rows, prompt), 0)
    pre_bias[...] = jnp.where(key_at <= query_at, 0.0, MASKED)
    key_at = lax.broadcasted_iota(jnp.int32, dec_bias.shape, 1)
    own_at = prompt + lax.broadcasted_iota(jnp.int32, dec_bias.shape, 0)
    diagonal = lax.broadcasted_iota(jnp.int32, (samples, samples), 0)
    diagonal = diagonal == lax.broadcasted_iota(jnp.int32, (samples, samples), 1)
    spread_len = jnp.broadcast_to(len_ref[...].astype(F32), (samples, samples))
    length = jnp.sum(jnp.where(diagonal, spread_len, 0.0), axis=1, keepdims=True)
    dec_bias[...] = jnp.where((key_at < length.astype(jnp.int32)) | (key_at == own_at), 0.0, MASKED)

    keys[...] = jnp.zeros_like(keys)
    keys[prompt : prompt + samples, 0:lat_width] = own_ref[...]
    for d in range(ns):
        for j in range(nx):
            at = lax.rem(z - d + ns, ns) * nh + lax.rem(core_peer - 2 * j + nh, nh)
            received(lat.at[at], c_recv.at[d, j], c_send.at[d, j], {"head": core_peer})
    for i in range(ns * nh):
        keys[i * block : (i + 1) * block, 0:lat_width] = lat[i]
    keys_t[...] = keys[...].T

    upv_copy.wait()
    dec_heads = cfg["dec_heads"]

    def decode_group(g, carry):
        at = pl.multiple_of(g * dec_heads * samples, 16)
        latent = softmax_latent(
            dec_abs[pl.ds(at, dec_heads * samples), :],
            keys_t[...],
            keys[:, 0:kv],
            dec_bias[...],
            scale,
        )
        for i in range(dec_heads):
            h = g * dec_heads + i
            one = jnp.dot(
                latent[i * samples : (i + 1) * samples], upv[h], preferred_element_type=F32
            )
            heads[z, :, pl.ds(pl.multiple_of(h * vdim, vdim), vdim)] = one.astype(BF16)
        return carry

    lax.fori_loop(0, hc // dec_heads, decode_group, 0)
    for d in order:
        slot = heads.at[z]
        send(slot, slot, h_send.at[d], h_recv.at[d], {"seq": seq_peer(d)})

    pre_heads = cfg["pre_heads"]
    groups = hc // pre_heads
    group_cols = pre_heads * vdim

    def prefill_group(g, carry):
        at = pl.multiple_of(g * pre_heads * rows, 16)
        latent = softmax_latent(
            pre_abs[pl.ds(at, pre_heads * rows), :],
            keys_t[:, 0:prompt],
            keys[0:prompt, 0:kv],
            pre_bias[...],
            scale,
        )
        for i in range(pre_heads):
            h = g * pre_heads + i
            one = jnp.dot(latent[i * rows : (i + 1) * rows], upv[h], preferred_element_type=F32)
            out[:, pl.ds(pl.multiple_of(h * vdim, vdim), vdim)] = one.astype(BF16)
        return carry

    first = groups // 2
    half_cols = first * group_cols
    lax.fori_loop(0, first, prefill_group, 0)
    front = pltpu.make_async_copy(
        out.at[:, pl.ds(0, half_cols)], out_hbm.at[:, pl.ds(0, half_cols)], out_sem.at[0]
    )
    front.start()

    proj_copy.wait()
    for d in order:
        at = lax.rem(z - d + ns, ns)
        received(heads.at[at], h_recv.at[d], h_send.at[d], {"seq": seq_peer(d)})
    cols = proj.shape[1]
    tile = cfg["tile"]
    share_rows = ns * samples // nh

    def project(n, carry):
        take = pl.ds(pl.multiple_of(n * tile, tile), tile)
        left = heads[...].reshape(ns * samples, hc * vdim)
        term = jnp.dot(left, proj[:, take], preferred_element_type=F32).astype(BF16)
        terms[:, :, take] = term.reshape(nh, share_rows, tile)
        return carry

    lax.fori_loop(0, cols // tile, project, 0)
    for d in range(1, nh):
        peer = head_peer(d)
        send(terms.at[peer], arrived.at[d], r_send.at[d], r_recv.at[d], {"head": peer})

    lax.fori_loop(first, groups, prefill_group, 0)
    back_cols = out.shape[1] - half_cols
    back = pltpu.make_async_copy(
        out.at[:, pl.ds(half_cols, back_cols)],
        out_hbm.at[:, pl.ds(half_cols, back_cols)],
        out_sem.at[1],
    )
    back.start()
    total = terms[hd].astype(F32)
    for d in range(1, nh):
        received(arrived.at[d], r_recv.at[d], r_send.at[d], {"head": core_peer})
        total = total + arrived[d].astype(F32)
    dec_ref[...] = total.astype(BF16)
    front.wait()
    back.wait()
    for copy in sent:
        copy.wait_send()


def fused_device(ns, nh, pq, lat, dq, own, length, upk, upv, proj):
    rows, hc, width = pq.shape
    samples = dq.shape[0]
    nope, kv = upk.shape[1:]
    vdim = upv.shape[2]
    block, lat_width = lat.shape
    prompt = ns * nh * block
    padded = round_up(lat_width, LANES)
    cols = proj.shape[1]
    share_rows = ns * samples // nh
    keys_rows = prompt + round_up(samples, LANES)
    nx = nh // 2
    dec_heads = max(1, min(hc, 512 // samples))
    pre_heads = max(1, min(hc // 2, 512 // rows))
    cfg = {
        "ns": ns,
        "nh": nh,
        "scale": width ** (-0.5),
        "chunks": 4,
        "dec_heads": dec_heads,
        "pre_heads": pre_heads,
        "tile": 256 if cols % 256 == 0 else LANES,
    }
    hbm = pl.BlockSpec(memory_space=pl.ANY)
    vmem = pl.BlockSpec(memory_space=pltpu.VMEM)
    dma = pltpu.SemaphoreType.DMA
    return pl.pallas_call(
        functools.partial(step_kernel, cfg),
        out_shape=(
            jax.ShapeDtypeStruct((rows, hc * vdim), BF16),
            jax.ShapeDtypeStruct((share_rows, cols), BF16),
        ),
        in_specs=[hbm, hbm, hbm, vmem, vmem, hbm, hbm, hbm],
        out_specs=(hbm, vmem),
        scratch_shapes=[
            pltpu.VMEM((hc, width, rows), BF16),
            pltpu.VMEM((samples, hc, width), BF16),
            pltpu.VMEM((ns * nh, block, lat_width), BF16),
            pltpu.VMEM((hc, nope, kv), BF16),
            pltpu.VMEM((hc, kv, vdim), BF16),
            pltpu.VMEM(proj.shape, BF16),
            pltpu.VMEM((samples * hc, nope), F32),
            pltpu.VMEM((samples * hc, LANES), F32),
            pltpu.VMEM((rows * hc, padded), BF16),
            pltpu.VMEM((samples * hc, padded), BF16),
            pltpu.VMEM((keys_rows, padded), BF16),
            pltpu.VMEM((padded, keys_rows), BF16),
            pltpu.VMEM((rows, prompt), F32),
            pltpu.VMEM((samples, keys_rows), F32),
            pltpu.VMEM((ns, samples, hc * vdim), BF16),
            pltpu.VMEM((rows, hc * vdim), BF16),
            pltpu.VMEM((nh, share_rows, cols), BF16),
            pltpu.VMEM((nh, share_rows, cols), BF16),
            dma,
            dma,
            dma,
            dma((cfg["chunks"],)),
            dma,
            dma,
            dma((2,)),
            dma((ns,)),
            dma((ns,)),
            dma((ns, nx)),
            dma((ns, nx)),
            dma((ns, nx)),
            dma((ns, nx)),
            dma((ns,)),
            dma((ns,)),
            dma((nh,)),
            dma((nh,)),
        ],
        compiler_params=pltpu.CompilerParams(
            collective_id=0, has_side_effects=True, vmem_limit_bytes=62 * 1024 * 1024
        ),
        name="rollout_step",
    )(jnp.transpose(pq, (1, 2, 0)), lat, dq, own, length.reshape(1, samples), upk, upv, proj)


def per_device(ns, nh, *args):
    pq, lat, dq, own, length, upk, upv, proj = args
    samples, hc = dq.shape[:2]
    fits = (
        lat.shape[0] % 16 == 0
        and nh % 2 == 0
        and ns > 1
        and hc % 8 == 0
        and pq.shape[0] % 16 == 0
        and samples % 16 == 0
        and (ns * samples) % (nh * 16) == 0
        and upk.shape[1] == LANES
        and upk.shape[2] % LANES == 0
        and upv.shape[2] == LANES
        and proj.shape[1] % LANES == 0
        and (ns * nh * lat.shape[0]) % LANES == 0
    )
    if fits:
        return tuple(fused_device(ns, nh, *args))
    return plain_device(*args)


def solution(mesh):
    in_specs = (
        P(("groups", "seq"), "head", None),
        P(("groups", "seq", "head"), None),
        P(("groups", "seq"), "head", None),
        P(("groups", "seq"), None),
        P(("groups", "seq")),
        P("head", None, None),
        P("head", None, None),
        P("head", "seq"),
    )
    out_specs = (P(("groups", "seq"), "head"), P(("groups", "head"), "seq"))
    return jax.shard_map(
        functools.partial(per_device, mesh.shape["seq"], mesh.shape["head"]),
        mesh=mesh, in_specs=in_specs,
        out_specs=out_specs,
        check_vma=False
    )
```

```python
import functools

import jax
import jax.numpy as jnp
from jax import lax
from jax.experimental import pallas as pl
from jax.experimental.pallas import tpu as pltpu
from jax.sharding import PartitionSpec as P


def absorb(query, up_key, nope_width):
    nope = jnp.einsum(
        "rhn,hnc->rhc", query[:, :, :nope_width], up_key, preferred_element_type=jnp.float32
    )
    return jnp.concatenate([nope.astype(jnp.bfloat16), query[:, :, nope_width:]], axis=2)


def fold_block(state, queries, piece, allowed_fn, kv_width, scale):
    peak, total, summed = state
    key_pos = jnp.arange(piece.shape[0], dtype=jnp.int32)
    allowed = allowed_fn(key_pos)
    scores = (
        lax.dot_general(
            queries, piece, (((1,), (1,)), ((), ())), preferred_element_type=jnp.float32
        )
        * scale
    )
    scores = jnp.where(allowed, scores, -1e30)
    new_peak = jnp.maximum(peak, jnp.max(scores, axis=1))
    weights = jnp.where(allowed, jnp.exp(scores - new_peak[:, None]), 0.0)
    factor = jnp.exp(peak - new_peak)
    total = total * factor + jnp.sum(weights, axis=1)
    summed = summed * factor[:, None] + jnp.dot(
        weights.astype(jnp.bfloat16), piece[:, :kv_width], preferred_element_type=jnp.float32
    )
    return (new_peak, total, summed)


def finish(state, rows, head_count, up_value):
    peak, total, summed = state
    latent = (summed / total[:, None]).astype(jnp.bfloat16).reshape(rows, head_count, -1)
    heads = jnp.einsum("rhc,hcv->rhv", latent, up_value, preferred_element_type=jnp.float32)
    return heads.astype(jnp.bfloat16).reshape(rows, -1)


def plain_device(
    prefill_query,
    prompt_latents,
    decode_query,
    sample_latent,
    sample_length,
    up_key,
    up_value,
    out_proj,
):
    local_rows, head_count, query_width = prefill_query.shape
    sample_rows = decode_query.shape[0]
    nope_width = up_key.shape[1]
    kv_width = up_key.shape[2]
    scale = query_width ** (-0.5)
    block = lax.all_gather(prompt_latents, "head", axis=0, tiled=True)
    prefill_rows = absorb(prefill_query, up_key, nope_width).reshape(local_rows * head_count, -1)
    first = lax.axis_index("seq") * local_rows
    query_pos = first + jnp.arange(local_rows * head_count, dtype=jnp.int32) // head_count
    decode_abs = absorb(decode_query, up_key, nope_width)
    decode_rows = decode_abs.reshape(sample_rows * head_count, -1)
    row_length = jnp.repeat(sample_length, head_count)
    own = (
        jnp.einsum(
            "rhc,rc->rh", decode_abs, sample_latent, preferred_element_type=jnp.float32
        ).reshape(-1)
        * scale
    )
    own_values = jnp.repeat(sample_latent[:, :kv_width].astype(jnp.float32), head_count, axis=0)
    count_prefill = local_rows * head_count
    prefill_init = (
        jnp.full((count_prefill,), -1e30, jnp.float32),
        jnp.zeros((count_prefill,), jnp.float32),
        jnp.zeros((count_prefill, kv_width), jnp.float32),
    )
    decode_init = (own, jnp.ones_like(own), own_values)

    def prefill_inner(state, piece):
        return fold_block(
            state,
            prefill_rows,
            piece,
            lambda key_pos: key_pos[None, :] <= query_pos[:, None],
            kv_width,
            scale,
        )

    def decode_inner(state, piece):
        return fold_block(
            state,
            decode_rows,
            piece,
            lambda key_pos: key_pos[None, :] < row_length[:, None],
            kv_width,
            scale,
        )

    def prefill_step(state, piece):
        return prefill_inner(state, piece)

    def decode_step(state, piece):
        return decode_inner(state, piece)

    state = (prefill_init, decode_init)
    piece = lax.all_gather(block, "seq", axis=0, tiled=True)
    prefill_state = prefill_step(state[0], piece)
    decode_state = decode_step(state[1], piece)
    prefill_heads = finish(prefill_state, local_rows, head_count, up_value)
    sample_heads = finish(decode_state, sample_rows, head_count, up_value)
    terms = jnp.dot(
        lax.all_gather(sample_heads, "seq", axis=0, tiled=True),
        out_proj,
        preferred_element_type=jnp.float32,
    )
    decode_out = lax.psum_scatter(
        terms.astype(jnp.bfloat16), "head", scatter_dimension=0, tiled=True
    )
    return (prefill_heads, decode_out)


LANES = 128
MASKED = -1e30
BF16 = jnp.bfloat16
F32 = jnp.float32


def round_up(value, unit):
    return -(-value // unit) * unit


def softmax_latent(queries, keys_t, values, bias, scale):
    rows = queries.shape[0]
    scores = jnp.dot(queries, keys_t, preferred_element_type=F32)
    per_head, key_count = bias.shape
    scores = (scores.reshape(rows // per_head, per_head, key_count) + bias[None]).reshape(
        rows, key_count
    )
    peak = jnp.max(scores, axis=1, keepdims=True)
    weights = jnp.exp((scores - peak) * scale)
    total = jnp.sum(weights, axis=1, keepdims=True)
    summed = jnp.dot(weights.astype(BF16), values, preferred_element_type=F32)
    return (summed * (1.0 / total)).astype(BF16)


def step_kernel(
    cfg,
    pq_hbm,
    lat_hbm,
    dq_hbm,
    own_ref,
    len_ref,
    upk_hbm,
    upv_hbm,
    proj_hbm,
    out_hbm,
    dec_ref,
    pq,
    dq,
    lat,
    upk,
    upv,
    proj,
    nope_rows,
    rope_rows,
    pre_abs,
    dec_abs,
    keys,
    keys_t,
    pre_bias,
    dec_bias,
    heads,
    out,
    partial,
    terms,
    arrived,
    pq_sem,
    dq_sem,
    lat_sem,
    upk_sem,
    upv_sem,
    proj_sem,
    out_sem,
    z_send,
    z_recv,
    x_send,
    x_recv,
    c_send,
    c_recv,
    h_send,
    h_recv,
    r_send,
    r_recv,
):
    ns, nh, scale = cfg["ns"], cfg["nh"], cfg["scale"]
    hc, width, rows = pq.shape
    samples = dq.shape[0]
    nope, kv = upk.shape[1], upk.shape[2]
    vdim = upv.shape[2]
    rope = width - nope
    lat_width = lat.shape[2]
    block = lat.shape[1]
    prompt = ns * nh * block
    padded = keys.shape[1]
    nx = nh // 2
    z, hd = lax.axis_index("seq"), lax.axis_index("head")
    core_peer = hd + 1 - 2 * lax.rem(hd, 2)

    def seq_peer(d):
        return lax.rem(z + d, ns)

    def head_peer(d):
        return lax.rem(hd + d, nh)

    copies = {}
    copies["pq"] = pltpu.make_async_copy(pq_hbm, pq, pq_sem)
    copies["dq"] = pltpu.make_async_copy(dq_hbm, dq, dq_sem)
    me_block = z * nh + hd
    copies["lat"] = pltpu.make_async_copy(lat_hbm, lat.at[me_block], lat_sem)
    chunks = cfg["chunks"]
    per_chunk = hc // chunks
    copies["lat"].start()
    copies["pq"].start()
    copies["dq"].start()
    upk_copies = [
        pltpu.make_async_copy(
            upk_hbm.at[pl.ds(c * per_chunk, per_chunk)],
            upk.at[pl.ds(c * per_chunk, per_chunk)],
            upk_sem.at[c],
        )
        for c in range(chunks)
    ]
    for copy in upk_copies:
        copy.start()
    upv_copy = pltpu.make_async_copy(upv_hbm, upv, upv_sem)
    upv_copy.start()
    proj_copy = pltpu.make_async_copy(proj_hbm, proj, proj_sem)
    proj_copy.start()

    barrier = pltpu.get_barrier_semaphore()
    for d in range(1, ns):
        pl.semaphore_signal(barrier, inc=1, device_id={"seq": seq_peer(d)})
    for d in range(1, nh):
        pl.semaphore_signal(barrier, inc=1, device_id={"head": head_peer(d)})
    pl.semaphore_wait(barrier, ns + nh - 2)

    sent = []

    def send(src, dst, send_sem, recv_sem, device):
        copy = pltpu.make_async_remote_copy(
            src_ref=src, dst_ref=dst, send_sem=send_sem, recv_sem=recv_sem, device_id=device
        )
        copy.start()
        sent.append(copy)

    def received(dst, recv_sem, send_sem, device):
        pltpu.make_async_remote_copy(
            src_ref=dst, dst_ref=dst, send_sem=send_sem, recv_sem=recv_sem, device_id=device
        ).wait_recv()

    def lat_block(d, j):
        return lax.rem(z - d + ns, ns) * nh + lax.rem(hd - 2 * j + nh, nh)

    def to_core(d, j):
        slot = lat.at[lat_block(d, j)]
        send(slot, slot, c_send.at[d, j], c_recv.at[d, j], {"head": core_peer})

    def to_x(d):
        slot = lat.at[lat_block(d, 0)]
        for j in range(1, nx):
            send(slot, slot, x_send.at[d, j], x_recv.at[d, j], {"head": head_peer(2 * j)})

    copies["lat"].wait()
    mine = lat.at[me_block]
    order = sorted(range(1, ns), key=lambda d: min(d, ns - d))
    for d in order:
        send(mine, mine, z_send.at[d], z_recv.at[d], {"seq": seq_peer(d)})
    to_x(0)
    to_core(0, 0)

    def take_z(d):
        received(lat.at[lat_block(d, 0)], z_recv.at[d], z_send.at[d], {"seq": seq_peer(d)})
        to_x(d)
        to_core(d, 0)

    def take_x(d):
        for j in range(1, nx):
            received(
                lat.at[lat_block(d, j)], x_recv.at[d, j], x_send.at[d, j], {"head": core_peer}
            )
            to_core(d, j)

    rope_rows[...] = jnp.zeros_like(rope_rows)
    pre_abs[:, kv:padded] = jnp.zeros((rows * hc, padded - kv), BF16)
    copies["dq"].wait()
    step = 8

    def spread(i, carry):
        piece = dq[pl.ds(i * step, step)].astype(F32)
        take = pl.ds(pl.multiple_of(i * step * hc, 8), step * hc)
        nope_rows[take, :] = piece[:, :, :nope].reshape(step * hc, nope)
        rope_rows[take, 0:rope] = piece[:, :, nope:].reshape(step * hc, rope)
        return carry

    lax.fori_loop(0, samples // step, spread, 0)
    copies["pq"].wait()

    def absorb_head(h, carry):
        query = pq[h].T
        take = pl.ds(h, samples, stride=hc)
        plain = jnp.concatenate([query[:, :nope], nope_rows[take, :].astype(BF16)], axis=0)
        turned = rope_rows[take, :].astype(BF16)
        absorbed = jnp.dot(plain, upk[h], preferred_element_type=F32).astype(BF16)
        at = pl.multiple_of(h * rows, 16)
        pre_abs[pl.ds(at, rows), 0:kv] = absorbed[:rows]
        pre_abs[pl.ds(at, rows), kv : kv + rope] = query[:, nope:]
        at = pl.multiple_of(h * samples, 16)
        dec_abs[pl.ds(at, samples), 0:kv] = absorbed[rows:]
        dec_abs[pl.ds(at, samples), kv:padded] = turned
        return carry

    pending = [functools.partial(take_z, d) for d in order]
    pending += [functools.partial(take_x, d) for d in [0] + order]
    share = -(-len(pending) // max(chunks - 1, 1))
    for c in range(chunks):
        upk_copies[c].wait()
        lax.fori_loop(c * per_chunk, (c + 1) * per_chunk, absorb_head, 0, unroll=2)
        for action in pending[:share]:
            action()
        pending = pending[share:]
    for action in pending:
        action()

    key_at = lax.broadcasted_iota(jnp.int32, (rows, prompt), 1)
    query_at = z * rows + lax.broadcasted_iota(jnp.int32, (rows, prompt), 0)
    pre_bias[...] = jnp.where(key_at <= query_at, 0.0, MASKED)
    key_at = lax.broadcasted_iota(jnp.int32, dec_bias.shape, 1)
    own_at = prompt + lax.broadcasted_iota(jnp.int32, dec_bias.shape, 0)
    diagonal = lax.broadcasted_iota(jnp.int32, (samples, samples), 0)
    diagonal = diagonal == lax.broadcasted_iota(jnp.int32, (samples, samples), 1)
    spread_len = jnp.broadcast_to(len_ref[...].astype(F32), (samples, samples))
    length = jnp.sum(jnp.where(diagonal, spread_len, 0.0), axis=1, keepdims=True)
    dec_bias[...] = jnp.where((key_at < length.astype(jnp.int32)) | (key_at == own_at), 0.0, MASKED)

    keys[...] = jnp.zeros_like(keys)
    keys[prompt : prompt + samples, 0:lat_width] = own_ref[...]
    for d in range(ns):
        for j in range(nx):
            at = lax.rem(z - d + ns, ns) * nh + lax.rem(core_peer - 2 * j + nh, nh)
            received(lat.at[at], c_recv.at[d, j], c_send.at[d, j], {"head": core_peer})
    for i in range(ns * nh):
        keys[i * block : (i + 1) * block, 0:lat_width] = lat[i]
    keys_t[...] = keys[...].T

    upv_copy.wait()
    dec_heads = cfg["dec_heads"]
    parts = hc // dec_heads

    for g in range(parts):
        at = g * dec_heads * samples
        latent = softmax_latent(
            dec_abs[at : at + dec_heads * samples, :],
            keys_t[...],
            keys[:, 0:kv],
            dec_bias[...],
            scale,
        )
        for i in range(dec_heads):
            one = jnp.dot(
                latent[i * samples : (i + 1) * samples],
                upv[g * dec_heads + i],
                preferred_element_type=F32,
            )
            heads[g, z, :, i * vdim : (i + 1) * vdim] = one.astype(BF16)
        slot = heads.at[g, z]
        for d in order[::-1]:
            send(slot, slot, h_send.at[g, d], h_recv.at[g, d], {"seq": seq_peer(d)})

    pre_heads = cfg["pre_heads"]
    groups = hc // pre_heads
    group_cols = pre_heads * vdim

    def prefill_group(g, carry):
        at = pl.multiple_of(g * pre_heads * rows, 16)
        latent = softmax_latent(
            pre_abs[pl.ds(at, pre_heads * rows), :],
            keys_t[:, 0:prompt],
            keys[0:prompt, 0:kv],
            pre_bias[...],
            scale,
        )
        for i in range(pre_heads):
            h = g * pre_heads + i
            one = jnp.dot(latent[i * rows : (i + 1) * rows], upv[h], preferred_element_type=F32)
            out[:, pl.ds(pl.multiple_of(h * vdim, vdim), vdim)] = one.astype(BF16)
        return carry

    first = groups - 1
    half_cols = first * group_cols
    lax.fori_loop(0, first, prefill_group, 0)
    front = pltpu.make_async_copy(
        out.at[:, pl.ds(0, half_cols)], out_hbm.at[:, pl.ds(0, half_cols)], out_sem.at[0]
    )
    front.start()

    proj_copy.wait()
    cols = proj.shape[1]
    tile = terms.shape[3]
    tiles = cols // tile
    share_rows = ns * samples // nh
    depth = dec_heads * vdim

    def product(g, n):
        left = heads[g].reshape(ns * samples, depth)
        right = proj[g * depth : (g + 1) * depth, pl.ds(pl.multiple_of(n * tile, tile), tile)]
        return jnp.dot(left, right, preferred_element_type=F32)

    for g in range(parts):
        for d in order:
            at = lax.rem(z - d + ns, ns)
            received(heads.at[g, at], h_recv.at[g, d], h_send.at[g, d], {"seq": seq_peer(d)})
        if g < parts - 1:

            def project(n, carry, g=g):
                value = product(g, n)
                partial[n] = value if g == 0 else partial[n] + value
                return carry

            lax.fori_loop(0, tiles, project, 0)
    for n in range(tiles):
        value = product(parts - 1, n)
        if parts > 1:
            value = partial[n] + value
        terms[n] = value.astype(BF16).reshape(nh, share_rows, tile)
        for d in range(1, nh):
            peer = head_peer(d)
            send(
                terms.at[n, peer],
                arrived.at[n, d],
                r_send.at[n, d],
                r_recv.at[n, d],
                {"head": peer},
            )

    lax.fori_loop(first, groups, prefill_group, 0)
    back_cols = out.shape[1] - half_cols
    back = pltpu.make_async_copy(
        out.at[:, pl.ds(half_cols, back_cols)],
        out_hbm.at[:, pl.ds(half_cols, back_cols)],
        out_sem.at[1],
    )
    back.start()
    for n in range(tiles):
        total = terms[n, hd].astype(F32)
        for d in range(1, nh):
            received(
                arrived.at[n, d], r_recv.at[n, d], r_send.at[n, d], {"head": core_peer}
            )
            total = total + arrived[n, d].astype(F32)
        dec_ref[:, n * tile : (n + 1) * tile] = total.astype(BF16)
    front.wait()
    back.wait()
    for copy in sent:
        copy.wait_send()


def fused_device(ns, nh, pq, lat, dq, own, length, upk, upv, proj):
    rows, hc, width = pq.shape
    samples = dq.shape[0]
    nope, kv = upk.shape[1:]
    vdim = upv.shape[2]
    block, lat_width = lat.shape
    prompt = ns * nh * block
    padded = round_up(lat_width, LANES)
    cols = proj.shape[1]
    share_rows = ns * samples // nh
    keys_rows = prompt + round_up(samples, LANES)
    nx = nh // 2
    dec_heads = max(1, min(hc, 256 // samples))
    parts = hc // dec_heads
    tile = 256 if cols % 256 == 0 else LANES
    tiles = cols // tile
    pre_heads = max(1, min(hc // 2, 512 // rows))
    cfg = {
        "ns": ns,
        "nh": nh,
        "scale": width ** (-0.5),
        "chunks": 4,
        "dec_heads": dec_heads,
        "pre_heads": pre_heads,
    }
    hbm = pl.BlockSpec(memory_space=pl.ANY)
    vmem = pl.BlockSpec(memory_space=pltpu.VMEM)
    dma = pltpu.SemaphoreType.DMA
    return pl.pallas_call(
        functools.partial(step_kernel, cfg),
        out_shape=(
            jax.ShapeDtypeStruct((rows, hc * vdim), BF16),
            jax.ShapeDtypeStruct((share_rows, cols), BF16),
        ),
        in_specs=[hbm, hbm, hbm, vmem, vmem, hbm, hbm, hbm],
        out_specs=(hbm, vmem),
        scratch_shapes=[
            pltpu.VMEM((hc, width, rows), BF16),
            pltpu.VMEM((samples, hc, width), BF16),
            pltpu.VMEM((ns * nh, block, lat_width), BF16),
            pltpu.VMEM((hc, nope, kv), BF16),
            pltpu.VMEM((hc, kv, vdim), BF16),
            pltpu.VMEM(proj.shape, BF16),
            pltpu.VMEM((samples * hc, nope), F32),
            pltpu.VMEM((samples * hc, LANES), F32),
            pltpu.VMEM((rows * hc, padded), BF16),
            pltpu.VMEM((samples * hc, padded), BF16),
            pltpu.VMEM((keys_rows, padded), BF16),
            pltpu.VMEM((padded, keys_rows), BF16),
            pltpu.VMEM((rows, prompt), F32),
            pltpu.VMEM((samples, keys_rows), F32),
            pltpu.VMEM((parts, ns, samples, dec_heads * vdim), BF16),
            pltpu.VMEM((rows, hc * vdim), BF16),
            pltpu.VMEM((tiles, ns * samples, tile), F32),
            pltpu.VMEM((tiles, nh, share_rows, tile), BF16),
            pltpu.VMEM((tiles, nh, share_rows, tile), BF16),
            dma,
            dma,
            dma,
            dma((cfg["chunks"],)),
            dma,
            dma,
            dma((2,)),
            dma((ns,)),
            dma((ns,)),
            dma((ns, nx)),
            dma((ns, nx)),
            dma((ns, nx)),
            dma((ns, nx)),
            dma((parts, ns)),
            dma((parts, ns)),
            dma((tiles, nh)),
            dma((tiles, nh)),
        ],
        compiler_params=pltpu.CompilerParams(
            collective_id=0, has_side_effects=True, vmem_limit_bytes=62 * 1024 * 1024
        ),
        name="rollout_step",
    )(jnp.transpose(pq, (1, 2, 0)), lat, dq, own, length.reshape(1, samples), upk, upv, proj)


def per_device(ns, nh, *args):
    pq, lat, dq, own, length, upk, upv, proj = args
    samples, hc = dq.shape[:2]
    fits = (
        lat.shape[0] % 16 == 0
        and nh % 2 == 0
        and ns > 1
        and hc % 8 == 0
        and hc % max(1, 256 // samples) == 0
        and pq.shape[0] % 16 == 0
        and samples % 16 == 0
        and (ns * samples) % (nh * 16) == 0
        and upk.shape[1] == LANES
        and upk.shape[2] % LANES == 0
        and upv.shape[2] == LANES
        and proj.shape[1] % LANES == 0
        and (ns * nh * lat.shape[0]) % LANES == 0
    )
    if fits:
        return tuple(fused_device(ns, nh, *args))
    return plain_device(*args)


def solution(mesh):
    in_specs = (
        P(("groups", "seq"), "head", None),
        P(("groups", "seq", "head"), None),
        P(("groups", "seq"), "head", None),
        P(("groups", "seq"), None),
        P(("groups", "seq")),
        P("head", None, None),
        P("head", None, None),
        P("head", "seq"),
    )
    out_specs = (P(("groups", "seq"), "head"), P(("groups", "head"), "seq"))
    return jax.shard_map(
        functools.partial(per_device, mesh.shape["seq"], mesh.shape["head"]),
        mesh=mesh, in_specs=in_specs,
        out_specs=out_specs,
        check_vma=False
    )
```

```python
import functools

import jax
import jax.numpy as jnp
from jax import lax
from jax.experimental import pallas as pl
from jax.experimental.pallas import tpu as pltpu
from jax.sharding import PartitionSpec as P


def absorb(query, up_key, nope_width):
    nope = jnp.einsum(
        "rhn,hnc->rhc", query[:, :, :nope_width], up_key, preferred_element_type=jnp.float32
    )
    return jnp.concatenate([nope.astype(jnp.bfloat16), query[:, :, nope_width:]], axis=2)


def fold_block(state, queries, piece, allowed_fn, kv_width, scale):
    peak, total, summed = state
    key_pos = jnp.arange(piece.shape[0], dtype=jnp.int32)
    allowed = allowed_fn(key_pos)
    scores = (
        lax.dot_general(
            queries, piece, (((1,), (1,)), ((), ())), preferred_element_type=jnp.float32
        )
        * scale
    )
    scores = jnp.where(allowed, scores, -1e30)
    new_peak = jnp.maximum(peak, jnp.max(scores, axis=1))
    weights = jnp.where(allowed, jnp.exp(scores - new_peak[:, None]), 0.0)
    factor = jnp.exp(peak - new_peak)
    total = total * factor + jnp.sum(weights, axis=1)
    summed = summed * factor[:, None] + jnp.dot(
        weights.astype(jnp.bfloat16), piece[:, :kv_width], preferred_element_type=jnp.float32
    )
    return (new_peak, total, summed)


def finish(state, rows, head_count, up_value):
    peak, total, summed = state
    latent = (summed / total[:, None]).astype(jnp.bfloat16).reshape(rows, head_count, -1)
    heads = jnp.einsum("rhc,hcv->rhv", latent, up_value, preferred_element_type=jnp.float32)
    return heads.astype(jnp.bfloat16).reshape(rows, -1)


def plain_device(
    prefill_query,
    prompt_latents,
    decode_query,
    sample_latent,
    sample_length,
    up_key,
    up_value,
    out_proj,
):
    local_rows, head_count, query_width = prefill_query.shape
    sample_rows = decode_query.shape[0]
    nope_width = up_key.shape[1]
    kv_width = up_key.shape[2]
    scale = query_width ** (-0.5)
    block = lax.all_gather(prompt_latents, "head", axis=0, tiled=True)
    prefill_rows = absorb(prefill_query, up_key, nope_width).reshape(local_rows * head_count, -1)
    first = lax.axis_index("seq") * local_rows
    query_pos = first + jnp.arange(local_rows * head_count, dtype=jnp.int32) // head_count
    decode_abs = absorb(decode_query, up_key, nope_width)
    decode_rows = decode_abs.reshape(sample_rows * head_count, -1)
    row_length = jnp.repeat(sample_length, head_count)
    own = (
        jnp.einsum(
            "rhc,rc->rh", decode_abs, sample_latent, preferred_element_type=jnp.float32
        ).reshape(-1)
        * scale
    )
    own_values = jnp.repeat(sample_latent[:, :kv_width].astype(jnp.float32), head_count, axis=0)
    count_prefill = local_rows * head_count
    prefill_init = (
        jnp.full((count_prefill,), -1e30, jnp.float32),
        jnp.zeros((count_prefill,), jnp.float32),
        jnp.zeros((count_prefill, kv_width), jnp.float32),
    )
    decode_init = (own, jnp.ones_like(own), own_values)

    def prefill_inner(state, piece):
        return fold_block(
            state,
            prefill_rows,
            piece,
            lambda key_pos: key_pos[None, :] <= query_pos[:, None],
            kv_width,
            scale,
        )

    def decode_inner(state, piece):
        return fold_block(
            state,
            decode_rows,
            piece,
            lambda key_pos: key_pos[None, :] < row_length[:, None],
            kv_width,
            scale,
        )

    def prefill_step(state, piece):
        return prefill_inner(state, piece)

    def decode_step(state, piece):
        return decode_inner(state, piece)

    state = (prefill_init, decode_init)
    piece = lax.all_gather(block, "seq", axis=0, tiled=True)
    prefill_state = prefill_step(state[0], piece)
    decode_state = decode_step(state[1], piece)
    prefill_heads = finish(prefill_state, local_rows, head_count, up_value)
    sample_heads = finish(decode_state, sample_rows, head_count, up_value)
    terms = jnp.dot(
        lax.all_gather(sample_heads, "seq", axis=0, tiled=True),
        out_proj,
        preferred_element_type=jnp.float32,
    )
    decode_out = lax.psum_scatter(
        terms.astype(jnp.bfloat16), "head", scatter_dimension=0, tiled=True
    )
    return (prefill_heads, decode_out)


LANES = 128
MASKED = -1e30
BF16 = jnp.bfloat16
F32 = jnp.float32


def round_up(value, unit):
    return -(-value // unit) * unit


def softmax_latent(queries, keys_t, values, bias, scale):
    rows = queries.shape[0]
    scores = jnp.dot(queries, keys_t, preferred_element_type=F32)
    per_head, key_count = bias.shape
    scores = (scores.reshape(rows // per_head, per_head, key_count) + bias[None]).reshape(
        rows, key_count
    )
    peak = jnp.max(scores, axis=1, keepdims=True)
    weights = jnp.exp((scores - peak) * scale)
    total = jnp.sum(weights, axis=1, keepdims=True)
    summed = jnp.dot(weights.astype(BF16), values, preferred_element_type=F32)
    return (summed * (1.0 / total)).astype(BF16)


def step_kernel(
    cfg,
    pq_hbm,
    lat_hbm,
    dq_hbm,
    own_ref,
    len_ref,
    upk_hbm,
    upv_hbm,
    proj_hbm,
    out_hbm,
    dec_ref,
    pq,
    dq,
    lat,
    upk,
    upv,
    proj,
    nope_rows,
    rope_rows,
    pre_abs,
    dec_abs,
    keys,
    keys_t,
    pre_bias,
    dec_bias,
    heads,
    out,
    partial,
    terms,
    arrived,
    pq_sem,
    dq_sem,
    lat_sem,
    upk_sem,
    upv_sem,
    proj_sem,
    out_sem,
    z_send,
    z_recv,
    x_send,
    x_recv,
    c_send,
    c_recv,
    h_send,
    h_recv,
    r_send,
    r_recv,
):
    ns, nh, scale = cfg["ns"], cfg["nh"], cfg["scale"]
    hc, width, rows = pq.shape
    samples = dq.shape[0]
    nope, kv = upk.shape[1], upk.shape[2]
    vdim = upv.shape[2]
    rope = width - nope
    lat_width = lat.shape[2]
    block = lat.shape[1]
    prompt = ns * nh * block
    padded = keys.shape[1]
    nx = nh // 2
    z, hd = lax.axis_index("seq"), lax.axis_index("head")
    core_peer = hd + 1 - 2 * lax.rem(hd, 2)

    def seq_peer(d):
        return lax.rem(z + d, ns)

    def head_peer(d):
        return lax.rem(hd + d, nh)

    copies = {}
    copies["pq"] = pltpu.make_async_copy(pq_hbm, pq, pq_sem)
    copies["dq"] = pltpu.make_async_copy(dq_hbm, dq, dq_sem)
    me_block = z * nh + hd
    copies["lat"] = pltpu.make_async_copy(lat_hbm, lat.at[me_block], lat_sem)
    chunks = cfg["chunks"]
    per_chunk = hc // chunks
    copies["lat"].start()
    copies["pq"].start()
    copies["dq"].start()
    upk_copies = [
        pltpu.make_async_copy(
            upk_hbm.at[pl.ds(c * per_chunk, per_chunk)],
            upk.at[pl.ds(c * per_chunk, per_chunk)],
            upk_sem.at[c],
        )
        for c in range(chunks)
    ]
    for copy in upk_copies:
        copy.start()
    upv_copy = pltpu.make_async_copy(upv_hbm, upv, upv_sem)
    upv_copy.start()
    proj_copy = pltpu.make_async_copy(proj_hbm, proj, proj_sem)
    proj_copy.start()

    barrier = pltpu.get_barrier_semaphore()
    for d in range(1, ns):
        pl.semaphore_signal(barrier, inc=1, device_id={"seq": seq_peer(d)})
    for d in range(1, nh):
        pl.semaphore_signal(barrier, inc=1, device_id={"head": head_peer(d)})
    pl.semaphore_wait(barrier, ns + nh - 2)

    sent = []

    def send(src, dst, send_sem, recv_sem, device):
        copy = pltpu.make_async_remote_copy(
            src_ref=src, dst_ref=dst, send_sem=send_sem, recv_sem=recv_sem, device_id=device
        )
        copy.start()
        sent.append(copy)

    def received(dst, recv_sem, send_sem, device):
        pltpu.make_async_remote_copy(
            src_ref=dst, dst_ref=dst, send_sem=send_sem, recv_sem=recv_sem, device_id=device
        ).wait_recv()

    def lat_block(d, j):
        return lax.rem(z - d + ns, ns) * nh + lax.rem(hd - 2 * j + nh, nh)

    def to_core(d, j):
        slot = lat.at[lat_block(d, j)]
        send(slot, slot, c_send.at[d, j], c_recv.at[d, j], {"head": core_peer})

    def to_x(d):
        slot = lat.at[lat_block(d, 0)]
        for j in range(1, nx):
            send(slot, slot, x_send.at[d, j], x_recv.at[d, j], {"head": head_peer(2 * j)})

    copies["lat"].wait()
    mine = lat.at[me_block]
    order = sorted(range(1, ns), key=lambda d: min(d, ns - d))
    for d in order:
        send(mine, mine, z_send.at[d], z_recv.at[d], {"seq": seq_peer(d)})
    to_x(0)
    to_core(0, 0)

    def take_z(d):
        received(lat.at[lat_block(d, 0)], z_recv.at[d], z_send.at[d], {"seq": seq_peer(d)})
        to_x(d)
        to_core(d, 0)

    def take_x(d):
        for j in range(1, nx):
            received(
                lat.at[lat_block(d, j)], x_recv.at[d, j], x_send.at[d, j], {"head": core_peer}
            )
            to_core(d, j)

    rope_rows[...] = jnp.zeros_like(rope_rows)
    pre_abs[:, kv:padded] = jnp.zeros((rows * hc, padded - kv), BF16)
    copies["dq"].wait()
    step = 8

    def spread(i, carry):
        piece = dq[pl.ds(i * step, step)].astype(F32)
        take = pl.ds(pl.multiple_of(i * step * hc, 8), step * hc)
        nope_rows[take, :] = piece[:, :, :nope].reshape(step * hc, nope)
        rope_rows[take, 0:rope] = piece[:, :, nope:].reshape(step * hc, rope)
        return carry

    lax.fori_loop(0, samples // step, spread, 0)
    copies["pq"].wait()

    def absorb_head(h, carry):
        query = pq[h].T
        take = pl.ds(h, samples, stride=hc)
        plain = jnp.concatenate([query[:, :nope], nope_rows[take, :].astype(BF16)], axis=0)
        turned = rope_rows[take, :].astype(BF16)
        absorbed = jnp.dot(plain, upk[h], preferred_element_type=F32).astype(BF16)
        at = pl.multiple_of(h * rows, 16)
        pre_abs[pl.ds(at, rows), 0:kv] = absorbed[:rows]
        pre_abs[pl.ds(at, rows), kv : kv + rope] = query[:, nope:]
        at = pl.multiple_of(h * samples, 16)
        dec_abs[pl.ds(at, samples), 0:kv] = absorbed[rows:]
        dec_abs[pl.ds(at, samples), kv:padded] = turned
        return carry

    pending = [functools.partial(take_z, d) for d in order]
    pending += [functools.partial(take_x, d) for d in [0] + order]
    share = -(-len(pending) // max(chunks - 1, 1))
    for c in range(chunks):
        upk_copies[c].wait()
        lax.fori_loop(c * per_chunk, (c + 1) * per_chunk, absorb_head, 0, unroll=2)
        for action in pending[:share]:
            action()
        pending = pending[share:]
    for action in pending:
        action()

    key_at = lax.broadcasted_iota(jnp.int32, (rows, prompt), 1)
    query_at = z * rows + lax.broadcasted_iota(jnp.int32, (rows, prompt), 0)
    pre_bias[...] = jnp.where(key_at <= query_at, 0.0, MASKED)
    key_at = lax.broadcasted_iota(jnp.int32, dec_bias.shape, 1)
    own_at = prompt + lax.broadcasted_iota(jnp.int32, dec_bias.shape, 0)
    diagonal = lax.broadcasted_iota(jnp.int32, (samples, samples), 0)
    diagonal = diagonal == lax.broadcasted_iota(jnp.int32, (samples, samples), 1)
    spread_len = jnp.broadcast_to(len_ref[...].astype(F32), (samples, samples))
    length = jnp.sum(jnp.where(diagonal, spread_len, 0.0), axis=1, keepdims=True)
    dec_bias[...] = jnp.where((key_at < length.astype(jnp.int32)) | (key_at == own_at), 0.0, MASKED)

    keys[...] = jnp.zeros_like(keys)
    keys[prompt : prompt + samples, 0:lat_width] = own_ref[...]
    for d in range(ns):
        for j in range(nx):
            at = lax.rem(z - d + ns, ns) * nh + lax.rem(core_peer - 2 * j + nh, nh)
            received(lat.at[at], c_recv.at[d, j], c_send.at[d, j], {"head": core_peer})
    for i in range(ns * nh):
        keys[i * block : (i + 1) * block, 0:lat_width] = lat[i]
    keys_t[...] = keys[...].T

    upv_copy.wait()
    dec_heads = cfg["dec_heads"]
    parts = hc // dec_heads

    for g in range(parts):
        at = g * dec_heads * samples
        latent = softmax_latent(
            dec_abs[at : at + dec_heads * samples, :],
            keys_t[...],
            keys[:, 0:kv],
            dec_bias[...],
            scale,
        )
        for i in range(dec_heads):
            one = jnp.dot(
                latent[i * samples : (i + 1) * samples],
                upv[g * dec_heads + i],
                preferred_element_type=F32,
            )
            heads[g, z, :, i * vdim : (i + 1) * vdim] = one.astype(BF16)
        slot = heads.at[g, z]
        for d in order[::-1]:
            send(slot, slot, h_send.at[g, d], h_recv.at[g, d], {"seq": seq_peer(d)})

    pre_heads = cfg["pre_heads"]
    groups = hc // pre_heads
    group_cols = pre_heads * vdim

    def prefill_group(g, carry):
        at = pl.multiple_of(g * pre_heads * rows, 16)
        latent = softmax_latent(
            pre_abs[pl.ds(at, pre_heads * rows), :],
            keys_t[:, 0:prompt],
            keys[0:prompt, 0:kv],
            pre_bias[...],
            scale,
        )
        for i in range(pre_heads):
            h = g * pre_heads + i
            one = jnp.dot(latent[i * rows : (i + 1) * rows], upv[h], preferred_element_type=F32)
            out[:, pl.ds(pl.multiple_of(h * vdim, vdim), vdim)] = one.astype(BF16)
        return carry

    first = groups - 1
    half_cols = first * group_cols
    lax.fori_loop(0, first, prefill_group, 0)
    front = pltpu.make_async_copy(
        out.at[:, pl.ds(0, half_cols)], out_hbm.at[:, pl.ds(0, half_cols)], out_sem.at[0]
    )
    front.start()

    proj_copy.wait()
    cols = proj.shape[1]
    tile = terms.shape[3]
    tiles = cols // tile
    share_rows = ns * samples // nh
    depth = dec_heads * vdim

    def product(g, n):
        left = heads[g].reshape(ns * samples, depth)
        right = proj[g * depth : (g + 1) * depth, pl.ds(pl.multiple_of(n * tile, tile), tile)]
        return jnp.dot(left, right, preferred_element_type=F32)

    for g in range(parts):
        for d in order:
            at = lax.rem(z - d + ns, ns)
            received(heads.at[g, at], h_recv.at[g, d], h_send.at[g, d], {"seq": seq_peer(d)})
        if g < parts - 1:

            def project(n, carry, g=g):
                value = product(g, n)
                partial[n] = value if g == 0 else partial[n] + value
                return carry

            lax.fori_loop(0, tiles, project, 0)
    for n in range(tiles):
        value = product(parts - 1, n)
        if parts > 1:
            value = partial[n] + value
        terms[n] = value.astype(BF16).reshape(nh, share_rows, tile)
        for j in range(nx):
            send(
                terms.at[n, lax.rem(core_peer + 2 * j, nh)],
                arrived.at[n, j],
                r_send.at[n, j],
                r_recv.at[n, j],
                {"head": core_peer},
            )
    for n in range(tiles):
        for j in range(nx):
            received(arrived.at[n, j], r_recv.at[n, j], r_send.at[n, j], {"head": core_peer})
            if j > 0:
                peer = head_peer(2 * j)
                pair = terms[n, peer].astype(F32) + arrived[n, j].astype(F32)
                terms[n, peer] = pair.astype(BF16)
                send(
                    terms.at[n, peer],
                    arrived.at[n, nx + j],
                    r_send.at[n, nx + j],
                    r_recv.at[n, nx + j],
                    {"head": peer},
                )

    lax.fori_loop(first, groups, prefill_group, 0)
    back_cols = out.shape[1] - half_cols
    back = pltpu.make_async_copy(
        out.at[:, pl.ds(half_cols, back_cols)],
        out_hbm.at[:, pl.ds(half_cols, back_cols)],
        out_sem.at[1],
    )
    back.start()
    for n in range(tiles):
        total = terms[n, hd].astype(F32) + arrived[n, 0].astype(F32)
        for d in range(nx + 1, nh):
            received(arrived.at[n, d], r_recv.at[n, d], r_send.at[n, d], {"head": core_peer})
            total = total + arrived[n, d].astype(F32)
        dec_ref[:, n * tile : (n + 1) * tile] = total.astype(BF16)
    front.wait()
    back.wait()
    for copy in sent:
        copy.wait_send()


def fused_device(ns, nh, pq, lat, dq, own, length, upk, upv, proj):
    rows, hc, width = pq.shape
    samples = dq.shape[0]
    nope, kv = upk.shape[1:]
    vdim = upv.shape[2]
    block, lat_width = lat.shape
    prompt = ns * nh * block
    padded = round_up(lat_width, LANES)
    cols = proj.shape[1]
    share_rows = ns * samples // nh
    keys_rows = prompt + round_up(samples, LANES)
    nx = nh // 2
    dec_heads = max(1, min(hc, 256 // samples))
    parts = hc // dec_heads
    tile = 256 if cols % 256 == 0 else LANES
    tiles = cols // tile
    pre_heads = max(1, min(hc // 2, 512 // rows))
    cfg = {
        "ns": ns,
        "nh": nh,
        "scale": width ** (-0.5),
        "chunks": 4,
        "dec_heads": dec_heads,
        "pre_heads": pre_heads,
    }
    hbm = pl.BlockSpec(memory_space=pl.ANY)
    vmem = pl.BlockSpec(memory_space=pltpu.VMEM)
    dma = pltpu.SemaphoreType.DMA
    return pl.pallas_call(
        functools.partial(step_kernel, cfg),
        out_shape=(
            jax.ShapeDtypeStruct((rows, hc * vdim), BF16),
            jax.ShapeDtypeStruct((share_rows, cols), BF16),
        ),
        in_specs=[hbm, hbm, hbm, vmem, vmem, hbm, hbm, hbm],
        out_specs=(hbm, vmem),
        scratch_shapes=[
            pltpu.VMEM((hc, width, rows), BF16),
            pltpu.VMEM((samples, hc, width), BF16),
            pltpu.VMEM((ns * nh, block, lat_width), BF16),
            pltpu.VMEM((hc, nope, kv), BF16),
            pltpu.VMEM((hc, kv, vdim), BF16),
            pltpu.VMEM(proj.shape, BF16),
            pltpu.VMEM((samples * hc, nope), F32),
            pltpu.VMEM((samples * hc, LANES), F32),
            pltpu.VMEM((rows * hc, padded), BF16),
            pltpu.VMEM((samples * hc, padded), BF16),
            pltpu.VMEM((keys_rows, padded), BF16),
            pltpu.VMEM((padded, keys_rows), BF16),
            pltpu.VMEM((rows, prompt), F32),
            pltpu.VMEM((samples, keys_rows), F32),
            pltpu.VMEM((parts, ns, samples, dec_heads * vdim), BF16),
            pltpu.VMEM((rows, hc * vdim), BF16),
            pltpu.VMEM((tiles, ns * samples, tile), F32),
            pltpu.VMEM((tiles, nh, share_rows, tile), BF16),
            pltpu.VMEM((tiles, nh, share_rows, tile), BF16),
            dma,
            dma,
            dma,
            dma((cfg["chunks"],)),
            dma,
            dma,
            dma((2,)),
            dma((ns,)),
            dma((ns,)),
            dma((ns, nx)),
            dma((ns, nx)),
            dma((ns, nx)),
            dma((ns, nx)),
            dma((parts, ns)),
            dma((parts, ns)),
            dma((tiles, nh)),
            dma((tiles, nh)),
        ],
        compiler_params=pltpu.CompilerParams(
            collective_id=0, has_side_effects=True, vmem_limit_bytes=62 * 1024 * 1024
        ),
        name="rollout_step",
    )(jnp.transpose(pq, (1, 2, 0)), lat, dq, own, length.reshape(1, samples), upk, upv, proj)


def per_device(ns, nh, *args):
    pq, lat, dq, own, length, upk, upv, proj = args
    samples, hc = dq.shape[:2]
    fits = (
        lat.shape[0] % 16 == 0
        and nh % 2 == 0
        and ns > 1
        and hc % 8 == 0
        and hc % max(1, 256 // samples) == 0
        and pq.shape[0] % 16 == 0
        and samples % 16 == 0
        and (ns * samples) % (nh * 16) == 0
        and upk.shape[1] == LANES
        and upk.shape[2] % LANES == 0
        and upv.shape[2] == LANES
        and proj.shape[1] % LANES == 0
        and (ns * nh * lat.shape[0]) % LANES == 0
    )
    if fits:
        return tuple(fused_device(ns, nh, *args))
    return plain_device(*args)


def solution(mesh):
    in_specs = (
        P(("groups", "seq"), "head", None),
        P(("groups", "seq", "head"), None),
        P(("groups", "seq"), "head", None),
        P(("groups", "seq"), None),
        P(("groups", "seq")),
        P("head", None, None),
        P("head", None, None),
        P("head", "seq"),
    )
    out_specs = (P(("groups", "seq"), "head"), P(("groups", "head"), "seq"))
    return jax.shard_map(
        functools.partial(per_device, mesh.shape["seq"], mesh.shape["head"]),
        mesh=mesh, in_specs=in_specs,
        out_specs=out_specs,
        check_vma=False
    )
```
